32 devices in a mesh: row: 4 (over x, core), col: 8 (over z, y).
Axes of the slice: x: 2, y: 2, z: 4, core: 2. Of those that a mesh axis runs over, the one named last changes fastest.
Arguments:
- centres: float32 [65536, 64], P(('row', 'col')), may hold values from -6 to 6
- weights: float32 [65536, 64], P(('row', 'col')), may hold values from -0.25 to 0.25
- targets: float32 [512, 64], replicated, may hold values from -6 to 6
- batch_index: int32 [512], replicated, may hold values from 0 to 65535
- nystrom_index: int32 [4096], replicated, may hold values from 0 to 65535
- eigvecs: float32 [4096, 1024], P('row', 'col'), may hold values from -0.09375 to 0.09375
- mode_scale: float32 [1024], P('col'), may hold values from 0.02 to 0.2
Outputs:
- residual: float32 [512, 64], replicated
- step: float32 [65536, 64], P(('row', 'col'))
The draws below stay inside these ranges and needn't reach their ends.
All inputs are finite; a program needn't handle non-finite values.
Results may differ from the reference program's by a relative error of at most 0.0001.
Values sent between devices are 32-bit elements; how exact they have to be, the bound alone decides.
A program may use at most 128 MiB of HBM per device.

```python
import math
import jax
import jax.numpy as jnp
from jax import lax

F = 64
O = 64
M = 4096
Q = 1024
B = 512
P_DEV = 2048
CENTRES = 65536


def set_ends(result, stream_key, least, top_value):
    shape = result.shape
    spot = [jax.random.randint(jax.random.fold_in(stream_key, axis), (), 0, shape[axis]) for axis in range(len(shape))]
    result = result.at[tuple(spot)].set(least)
    longest = shape.index(max(shape))
    spot[longest] = (spot[longest] + 1) % shape[longest]
    return result.at[tuple(spot)].set(top_value)


def level_of(key, dims, cuts, low, top_value):
    def one(axis_at, parts):
        steps = jax.random.uniform(jax.random.fold_in(jax.random.fold_in(key, 6), axis_at), (parts,), jnp.float32, low / len(cuts), top_value / len(cuts))
        return jnp.repeat(jnp.exp(steps), dims[axis_at] // parts).reshape((-1,) + (1,) * (len(dims) - axis_at - 1))

    level = one(*cuts[0])
    for cut in cuts[1:]:
        level = level * one(*cut)
    return level


def gaussian(key, shape, deviation, reach, pieces=(), dtype=jnp.bfloat16):
    result = deviation * jax.random.normal(key, shape, jnp.float32)
    if pieces:
        result = result * level_of(key, shape, pieces, -0.22, 0.18)
    return jnp.clip(result, -reach, reach).astype(dtype)


def setup_inputs(seed: int = 0) -> dict:
    streams_of = jax.random.split(jax.random.key(seed), 8)
    centres = gaussian(streams_of[0], (CENTRES, F), 1.0, 6.0, ((0, 32),), jnp.float32)
    weights = gaussian(streams_of[1], (CENTRES, O), (4.0 / CENTRES ** 0.5), 0.25, ((0, 32),), jnp.float32)
    targets = gaussian(streams_of[2], (B, O), 1.0, 6.0, (), jnp.float32)
    batch_index = set_ends(jax.random.randint(streams_of[3], (B,), 0, CENTRES), jax.random.fold_in(streams_of[3], 1), 0, CENTRES - 1).astype(jnp.int32)
    nystrom_index = set_ends(jax.random.randint(streams_of[4], (M,), 0, CENTRES), jax.random.fold_in(streams_of[4], 1), 0, CENTRES - 1).astype(jnp.int32)
    eigvecs = gaussian(streams_of[5], (M, Q), M ** -0.5, 0.09375, ((0, 4), (1, 8)), jnp.float32)
    mode_scale = jnp.clip(jnp.exp(math.log(0.2) - 2.3025851 * jax.random.uniform(streams_of[6], (Q,), jnp.float32) ** level_of(streams_of[6], (Q,), ((0, 8),), -0.2, 0.2)), 0.02, 0.2)
    return {"centres": centres, "weights": weights, "targets": targets, "batch_index": batch_index, "nystrom_index": nystrom_index, "eigvecs": eigvecs, "mode_scale": mode_scale}


learning_rate = 0.25


def kernel(left, right):
    left_sq = jnp.sum(left * left, axis=1)
    right_sq = jnp.sum(right * right, axis=1)
    inner_prod = jnp.dot(left, right.T, precision=lax.Precision.HIGHEST, preferred_element_type=jnp.float32)
    return jnp.exp(-(left_sq[:, None] + right_sq[None, :] - 2.0 * inner_prod) / float(F))


def reference(centres, weights, targets, batch_index, nystrom_index, eigvecs, mode_scale):
    batch_feats = centres[batch_index]
    nystrom = centres[nystrom_index]
    blocks = CENTRES // P_DEV
    cent_blocks = centres.reshape(blocks, P_DEV, F)
    wts_blocks = weights.reshape(blocks, P_DEV, O)

    def add_block(running, pair):
        cent_blk, wts_blk = pair
        kern_tile = kernel(cent_blk, batch_feats)
        return running + jnp.dot(kern_tile.T, wts_blk, precision=lax.Precision.HIGHEST, preferred_element_type=jnp.float32), None

    prediction, unused = lax.scan(add_block, jnp.zeros((B, O), jnp.float32), (cent_blocks, wts_blocks))
    residual = prediction - targets
    gradient = jnp.dot(kernel(nystrom, batch_feats), residual, precision=lax.Precision.HIGHEST, preferred_element_type=jnp.float32)
    coeff = mode_scale[:, None] * jnp.dot(eigvecs.T, gradient, precision=lax.Precision.HIGHEST, preferred_element_type=jnp.float32)
    correction = jnp.dot(eigvecs, coeff, precision=lax.Precision.HIGHEST, preferred_element_type=jnp.float32)

    def step_block(cent_blk):
        direct = jnp.dot(kernel(cent_blk, batch_feats), residual, precision=lax.Precision.HIGHEST, preferred_element_type=jnp.float32)
        back = jnp.dot(kernel(cent_blk, nystrom), correction, precision=lax.Precision.HIGHEST, preferred_element_type=jnp.float32)
        return learning_rate * (direct - back)

    step = lax.map(step_block, cent_blocks).reshape(CENTRES, O)
    return residual, step
```

```python
import functools
import math

import jax
import jax.numpy as jnp
from jax import lax
from jax.experimental import pallas as pl
from jax.experimental.pallas import tpu as pltpu
from jax.sharding import PartitionSpec as P

learning_rate = 0.25
CORES = 2
HALVES = 2
MESH = pl.DeviceIdType.MESH
VMEM = pl.BlockSpec(memory_space=pltpu.VMEM)
BF16 = jnp.bfloat16
F32 = jnp.float32


def pieces(value, count):
    parts = []
    for step in range(count):
        part = value.astype(BF16).astype(F32)
        parts.append(part)
        value = value - part
    return parts


def paired(value):
    return jnp.concatenate(pieces(value, 2), axis=0).astype(BF16)


def augmented(feats, left):
    width, count = feats.shape
    unit = math.log2(math.e) / width
    square = pieces(-unit * jnp.sum(feats * feats, axis=0, keepdims=True), 3)
    if left:
        high, low = pieces(feats * (2.0 * unit), 2)
        parts, first, one = [high, low, high], 0, 3
    else:
        high, low = pieces(feats, 2)
        parts, first, one = [high, high, low], 3, 0
    spot = lax.broadcasted_iota(jnp.int32, (8, count), 0)
    tail = jnp.where((spot >= one) & (spot < one + 3), 1.0, 0.0)
    for at, part in enumerate(square):
        tail = jnp.where(spot == first + at, part, tail)
    deep = depth_of(width)
    fill = jnp.zeros((deep - 3 * width - 8, count), F32)
    return jnp.concatenate(parts + [tail, fill], axis=0)


def apply(value, eig_ref, how):
    count = value.shape[0]
    both = paired(value)
    wide = lax.dot_general(both, eig_ref[0], how, preferred_element_type=F32)
    slim = lax.dot_general(both[:count], eig_ref[1], how, preferred_element_type=F32)
    return wide[:count] + (wide[count:] + slim)


def depth_of(width):
    return -(-(3 * width + 8) // 128) * 128


def largest(count, limit):
    return max(d for d in range(1, limit + 1) if count % d == 0)


def kmul(a_ref, b_ref, w_ref, o_ref):
    points, outs = a_ref.shape[0], o_ref.shape[0]
    wide = b_ref.shape[1]
    sub = min(512, points)
    parts = largest(points // sub, 3)
    tile = min(512, wide)

    def across(i, unused):
        to = pl.ds(pl.multiple_of(i * tile, tile), tile)
        b = b_ref[:, to]

        def down(j, total):
            for part in range(parts):
                at = pl.ds(pl.multiple_of((j * parts + part) * sub, sub), sub)
                value = jnp.exp2(jnp.dot(a_ref[at, :], b, preferred_element_type=F32))
                high = value.astype(BF16)
                low = (value - high.astype(F32)).astype(BF16)
                w = w_ref[:, at]
                total = total + (
                    jnp.dot(w, high, preferred_element_type=F32)
                    + jnp.dot(w, low, preferred_element_type=F32)
                )
            return total

        total = lax.fori_loop(0, points // (sub * parts), down, jnp.zeros((2 * outs, tile), F32), unroll=True)
        o_ref[:, to] = total[:outs] + total[outs:]
        return unused

    lax.fori_loop(0, wide // tile, across, 0, unroll=True)


def split_of(xs, cs):
    ys = xs if cs % xs == 0 else 1
    return ys, cs // ys


class Place:
    def __init__(self, xs, cs):
        self.xs, self.cs = xs, cs
        self.ys, self.zs = split_of(xs, cs)
        row = lax.axis_index("row")
        self.c = lax.axis_index("col")
        self.k = lax.rem(row, CORES)
        self.x = row // CORES
        self.z, self.y = self.c // self.ys, lax.rem(self.c, self.ys)

    def device(self, k, x, c):
        return (x * CORES + k, c)

    def core(self):
        return [(1 - self.k, self.device(1 - self.k, self.x, self.c))]

    def line(self):
        spots = [lax.rem(self.x + d, self.xs) for d in range(1, self.xs)]
        return [(s, self.device(self.k, s, self.c)) for s in spots]

    def senders(self):
        return [lax.rem(self.x + self.xs - d, self.xs) for d in range(1, self.xs)]

    def cols(self):
        spots = [self.c ^ d for d in range(1, self.cs)]
        return [(s, self.device(self.k, self.x, s)) for s in spots]

    def plane(self):
        found = []
        for d in range(1, self.xs * self.ys):
            x = lax.rem(self.x + d // self.ys, self.xs)
            y = lax.rem(self.y + d % self.ys, self.ys)
            found.append(((x, y), self.device(self.k, x, self.z * self.ys + y)))
        return found

    def across(self):
        spots = [lax.rem(self.y + d, self.ys) for d in range(1, self.ys)]
        return [(s, self.device(self.k, self.x, self.z * self.ys + s)) for s in spots]

    def along(self):
        spots = [lax.rem(self.z + d, self.zs) for d in range(1, self.zs)]
        return [(s, self.device(self.k, self.x, s * self.ys + self.y)) for s in spots]

    def chips(self):
        found = []
        for d in range(1, self.xs * self.cs):
            x, c = lax.rem(self.x + d // self.cs, self.xs), self.c ^ (d % self.cs)
            found.append(((x, c), self.device(self.k, x, c)))
        return found

    def arrive(self):
        sem = pltpu.get_barrier_semaphore()
        everyone = self.core() + self.chips()
        for spot, device in everyone:
            pl.semaphore_signal(sem, inc=1, device_id=device, device_id_type=MESH)
        return lambda: pl.semaphore_wait(sem, len(everyone))


def start(partners, source, target, sems):
    copies = []
    for d, (spot, device) in enumerate(partners):
        copies.append(
            pltpu.make_async_remote_copy(
                src_ref=source(d, spot),
                dst_ref=target(d, spot),
                send_sem=sems[0],
                recv_sem=sems[1],
                device_id=device,
                device_id_type=MESH,
            )
        )
    for copy in copies:
        copy.start()
    return copies


def await_all(whole, sem):
    pltpu.make_async_copy(whole, whole, sem).wait()


def finish(whole, sems):
    for sem in sems:
        await_all(whole, sem)


def summed(first, buffers, count):
    total = first
    for d in range(count):
        total = total + buffers[d]
    return total


def everywhere_steps(place, bufs, sems):
    in_ref, by_core, on_core, by_chip, o_ref = bufs
    k, x, c = place.k, place.x, place.c
    start(place.core(), lambda d, s: in_ref.at[s], lambda d, s: by_core.at[d], sems[0])
    yield
    finish(by_core, sems[0])
    on_core[...] = in_ref[k] + by_core[0]
    start(place.chips(), lambda d, s: on_core.at[s], lambda d, s: by_chip.at[d], sems[1])
    yield
    finish(by_chip, sems[1])
    o_ref[k, x, c] = summed(on_core[x, c], by_chip, by_chip.shape[0])
    start(
        place.chips(), lambda d, s: o_ref.at[k, x, c], lambda d, s: o_ref.at[k, x, c], sems[2]
    )
    yield
    finish(by_chip, sems[2])
    start(place.core(), lambda d, s: o_ref.at[k], lambda d, s: o_ref.at[k], sems[3])
    yield
    finish(by_core, sems[3])


def point_steps(place, bufs, sems):
    in_ref, by_core, on_core, by_plane, on_plane, by_line, o_ref = bufs
    k, x, y, z = place.k, place.x, place.y, place.z
    start(place.core(), lambda d, s: in_ref.at[s], lambda d, s: by_core.at[d], sems[0])
    yield
    finish(by_core, sems[0])
    on_core[...] = in_ref[k] + by_core[0]
    start(place.plane(), lambda d, s: on_core.at[s], lambda d, s: by_plane.at[d], sems[1])
    yield
    finish(by_plane, sems[1])
    on_plane[...] = summed(on_core[x, y], by_plane, by_plane.shape[0])
    start(place.along(), lambda d, s: on_plane.at[s], lambda d, s: by_line.at[d], sems[2])
    yield
    finish(by_line, sems[2])
    o_ref[k, x, y, z] = summed(on_plane[z], by_line, place.zs - 1)
    piece = lambda d, s: o_ref.at[k, x, y, z]
    start(place.along(), piece, piece, sems[3])
    yield
    finish(by_line, sems[3])
    piece = lambda d, s: o_ref.at[k, x, y]
    start(place.across(), piece, piece, sems[4])
    yield
    finish(by_plane.at[pl.ds(0, place.ys - 1)], sems[4])
    piece = lambda d, s: o_ref.at[k, x]
    start(place.line(), piece, piece, sems[5])
    yield
    finish(on_core.at[pl.ds(0, place.xs - 1)], sems[5])
    piece = lambda d, s: o_ref.at[k]
    start(place.core(), piece, piece, sems[6])
    yield
    finish(by_core, sems[6])


def mode_steps(place, bufs, sems, scale_ref, eig_ref):
    part, by_core, on_core, by_line, terms, by_col, o_ref = bufs
    start(place.core(), lambda d, s: part, lambda d, s: by_core.at[d], sems[0])
    yield
    finish(by_core, sems[0])
    on_core[...] = part[...] + by_core[0]
    start(place.line(), lambda d, s: on_core, lambda d, s: by_line.at[d], sems[1])
    yield
    finish(by_line, sems[1])
    coeff = summed(on_core[...], by_line, place.xs - 1) * scale_ref[...]
    correction = apply(coeff, eig_ref, (((1,), (1,)), ((), ())))
    store_tiles(correction, 0, lambda t, tile: place_in(terms, t, tile))
    start(place.cols(), lambda d, s: terms.at[s], lambda d, s: by_col.at[d], sems[2])
    yield
    finish(by_col, sems[2])
    o_ref[place.k, place.x, place.c] = summed(terms[place.c], by_col, place.cs - 1)


def spread(place, o_ref, by_line, by_col, sems, use):
    k, x, c, cs = place.k, place.x, place.c, place.cs
    size = cs // HALVES
    own, own_sent, line, line_sent, near, near_sent, far, far_sent = sems
    halves = [c // size, 1 - c // size]
    part = lambda ref, at: ref.at[pl.ds(at * size, size)]

    def across(d):
        piece = lambda e, s: o_ref.at[k, x, c ^ d]
        start(place.line(), piece, piece, [line_sent.at[0], line.at[d // size]])

    def beside(ref, at, ends):
        piece = lambda d, s: part(ref, at)
        start(place.core(), piece, piece, ends)

    mine = [
        start([partner], lambda d, s: o_ref.at[k, x, c], lambda d, s: o_ref.at[k, x, c], [own_sent.at[0], own.at[d]])
        for d, partner in enumerate(place.cols())
    ]
    across(0)
    for h in range(HALVES):
        for d in range(max(1, h * size), (h + 1) * size):
            await_all(o_ref.at[k, x, c], own.at[d - 1])
            across(d)
        beside(o_ref.at[k, x], halves[h], [near_sent.at[0], near.at[h]])
    for h in range(HALVES):
        use(k, x, halves[h])
    for h in range(HALVES):
        await_all(part(o_ref.at[k, x], 0), near.at[h])
        use(1 - k, x, halves[h])
    for h in range(HALVES):
        await_all(by_line.at[:, pl.ds(0, size)], line.at[h])
        for spot in place.senders():
            beside(o_ref.at[k, spot], halves[h], [far_sent.at[0], far.at[h]])
        for spot in place.senders():
            use(k, spot, halves[h])
    for h in range(HALVES):
        await_all(by_line.at[:, pl.ds(0, size)], far.at[h])
        for spot in place.senders():
            use(1 - k, spot, halves[h])
    await_all(by_col, own_sent.at[0])
    await_all(by_line, line_sent.at[0])
    await_all(o_ref.at[k, x], near_sent.at[0])
    await_all(by_line, far_sent.at[0])


def spot_in(shape, t):
    spots = []
    for count in reversed(shape):
        t, spot = divmod(t, count)
        spots.append(spot)
    return t, tuple(reversed(spots))


def spot_of(shape, t):
    row, spots = spot_in(shape[2:-2], t)
    return (row % CORES, row // CORES) + spots


def place_in(terms, t, tile):
    terms[divmod(t, terms.shape[1])] = tile


def store_tiles(value, block, put):
    high = value.shape[0] // 8
    for j in range(value.shape[1] // 128):
        for g in range(high):
            put((block + j) * high + g, value[8 * g : 8 * g + 8, 128 * j : 128 * j + 128])


def store_all(buf, block, value):
    def put(t, tile):
        buf[spot_of(buf.shape, t)] = tile

    store_tiles(value, block, put)


def load_tiles(get, high, block, blocks):
    columns = []
    for j in range(block, block + blocks):
        columns.append(jnp.concatenate([get(j * high + g) for g in range(high)], axis=0))
    return jnp.concatenate(columns, axis=1) if blocks > 1 else columns[0]


def load_all(buf, high, block, blocks):
    return load_tiles(lambda t: buf[spot_of(buf.shape, t)], high, block, blocks)


def share_of(tiles, xs, cs):
    return -(-tiles // (CORES * xs * cs))


def everywhere_shapes(tiles, xs, cs):
    piece = (share_of(tiles, xs, cs), 8, 128)
    shapes = [
        (CORES, xs, cs) + piece,
        (1, xs, cs) + piece,
        (xs, cs) + piece,
        (xs * cs - 1,) + piece,
        (CORES, xs, cs) + piece,
    ]
    return [pltpu.VMEM(shape, F32) for shape in shapes]


def point_shapes(tiles, xs, cs):
    piece = (share_of(tiles, xs, cs), 8, 128)
    ys, zs = split_of(xs, cs)
    shapes = [
        (CORES, xs, ys, zs) + piece,
        (1, xs, ys, zs) + piece,
        (xs, ys, zs) + piece,
        (xs * ys - 1, zs) + piece,
        (zs,) + piece,
        (zs - 1,) + piece,
        (CORES, xs, ys, zs) + piece,
    ]
    return [pltpu.VMEM(shape, F32) for shape in shapes]


CHUNK = 512


def main_body(
    xs, cs, batch, points, centres_in, weights_in, targets_in, batch_in, points_in, scale_in, eig_in,
    residual, step, *scratch
):
    width, rows = centres_in.shape
    outs = targets_in.shape[0]
    block = eig_in.shape[0]
    some = block // HALVES
    high = width // 8
    scratch = list(scratch)
    take = lambda count: [scratch.pop(0) for i in range(count)]
    pair = lambda count: [[ref.at[0] for ref in take(2)] for i in range(count)]
    b_bufs, p_bufs, m_bufs = take(5), take(5), take(7)
    n_bufs = [take(7) for h in range(HALVES)]
    split, left_rows, batch_right, batch_left, block_high, block_low, pairs, pred = take(8)
    left, kern_high, kern_low = take(3)
    b_sems, p_sems, m_sems = pair(4), pair(4), pair(3)
    n_sems = [pair(7) for h in range(HALVES)]
    spread_sems, input_sems = take(8), take(1)[0]
    by_line = take(1)[0]
    inputs = take(7)
    eig_pair = take(1)[0]
    place = Place(xs, cs)
    k, x, c = place.k, place.x, place.c
    met = place.arrive()
    sources = [centres_in, weights_in, targets_in, batch_in, points_in, scale_in, eig_in]
    loads = [
        pltpu.make_async_copy(source, ref, input_sems.at[i])
        for i, (source, ref) in enumerate(zip(sources, inputs))
    ]
    for i in (0, 3, 4, 1, 2, 5, 6):
        loads[i].start()
    centres, weights, targets, batch_at, points_at, scale, eig = inputs
    offset = lax.axis_index(("row", "col")) * rows

    def pick(index):
        count = index.shape[1]
        spot = lax.broadcasted_iota(jnp.int32, (rows, count), 0)
        hot = jnp.where(spot == index - offset, 1.0, 0.0).astype(BF16)
        got = jnp.dot(split[...], hot, preferred_element_type=F32)
        return (got[:width] + got[width : 2 * width]) + got[2 * width :]

    def pick_points(h, first, last):
        groups = points // block
        for row in range(first * groups // 2, last * groups // 2):
            at = row * block + h * some
            store_all(n_bufs[h][0], row * some // 128, pick(points_at[:, at : at + some]))

    def keep_kernel(first, points_rows):
        count = points_rows.shape[0]
        tile = min(CHUNK, rows)

        def across(i, unused):
            to = pl.ds(pl.multiple_of(i * tile, tile), tile)
            value = jnp.exp2(jnp.dot(points_rows, left[:, to], preferred_element_type=F32))
            near = value.astype(BF16)
            kern_high[pl.ds(first, count), to] = near
            kern_low[pl.ds(first, count), to] = (value - near.astype(F32)).astype(BF16)
            return unused

        lax.fori_loop(0, rows // tile, across, 0, unroll=True)

    def fold(w, first, begin):
        tile = min(CHUNK, rows)
        rest = pl.ds(first, w.shape[1])

        def across(i, unused):
            to = pl.ds(pl.multiple_of(i * tile, tile), tile)
            total = jnp.dot(w, kern_high[rest, to], preferred_element_type=F32)
            total = total + jnp.dot(w, kern_low[rest, to], preferred_element_type=F32)
            total = total[:outs] + total[outs:]
            step[:, to] = total if begin else step[:, to] + total
            return unused

        lax.fori_loop(0, rows // tile, across, 0, unroll=True)

    def row_at(k, x, h):
        return batch + pl.multiple_of((x * CORES + k) * block + h * some, some)

    def feats_of(h, k, x):
        mine = n_bufs[h][6].at[k, x]
        return load_tiles(lambda t: mine[spot_in(mine.shape[:-2], t)[1]], high, 0, some // 128)

    def point_form(h, k, x):
        keep_kernel(row_at(k, x, h), augmented(feats_of(h, k, x), False).T.astype(BF16))

    def own_form(h):
        feats = feats_of(h, k, x)
        form = augmented(feats, False)
        keep_kernel(row_at(k, x, h), form.T.astype(BF16))
        to = slice(h * some, h * some + some)
        value = jnp.exp2(jnp.dot(batch_left[...], form.astype(BF16), preferred_element_type=F32))
        near = value.astype(BF16)
        block_high[:, to] = near
        block_low[:, to] = (value - near.astype(F32)).astype(BF16)

    def use(k, x, h):
        size = cs // HALVES
        mine = m_bufs[6].at[k, x, pl.ds(h * size, size)]
        correction = load_tiles(lambda t: mine[divmod(t, mine.shape[1])], outs // 8, 0, some // 128)
        fold(paired(-learning_rate * correction), row_at(k, x, h), False)

    for bufs in [b_bufs, p_bufs] + n_bufs:
        bufs[0][...] = jnp.zeros_like(bufs[0])
    loads[0].wait()
    loads[3].wait()
    split[...] = jnp.concatenate(pieces(centres[...], 3), axis=0).astype(BF16)
    for at in range(0, batch, CHUNK):
        store_all(b_bufs[0], at // 128, pick(batch_at[:, at : min(at + CHUNK, batch)]))
    loads[4].wait()
    met()
    of_batch = everywhere_steps(place, b_bufs, b_sems)
    of_pred = everywhere_steps(place, p_bufs, p_sems)
    of_points = [point_steps(place, n_bufs[h], n_sems[h]) for h in range(HALVES)]
    next(of_batch)
    pick_points(0, 0, 1)
    next(of_batch)
    pick_points(0, 1, 2)
    next(of_points[0])
    pick_points(1, 0, 2)
    next(of_points[1])
    next(of_points[0])
    next(of_batch)
    next(of_points[1])
    for at in range(0, rows, CHUNK):
        to = slice(at, min(at + CHUNK, rows))
        form = augmented(centres[:, to], True)
        left[:, to] = form.astype(BF16)
        left_rows[to, :] = form.T.astype(BF16)
    for i in (1, 2, 5, 6):
        loads[i].wait()
    pairs[...] = paired(weights[...])
    eig_pair[0], eig_pair[1] = [part.astype(BF16) for part in pieces(eig[...], 2)]
    next(of_points[0])
    next(of_batch)
    next(of_batch, None)

    feats = load_all(b_bufs[4], high, 0, batch // 128)
    form = augmented(feats, False)
    batch_right[...] = form.astype(BF16)
    kmul(left_rows, batch_right, pairs, pred)
    store_all(p_bufs[0], 0, pred[...])
    next(of_pred)
    next(of_points[0])
    next(of_points[1])
    batch_left[...] = augmented(feats, True).T.astype(BF16)
    next(of_pred)
    keep_kernel(0, form.T.astype(BF16))
    next(of_points[0])
    next(of_points[1])
    next(of_pred)
    next(of_points[0])
    own_form(0)
    next(of_points[1])
    next(of_points[1])
    own_form(1)
    next(of_pred)
    next(of_points[0])
    next(of_pred, None)

    rest = load_all(p_bufs[4], outs // 8, 0, batch // 128) - targets[...]
    residual[...] = rest
    pair_rest = paired(rest)
    grad = jnp.dot(pair_rest, block_high[...], preferred_element_type=F32)
    grad = grad + jnp.dot(pair_rest, block_low[...], preferred_element_type=F32)
    m_bufs[0][...] = apply(grad[:outs] + grad[outs:], eig_pair, (((1,), (0,)), ((), ())))
    of_modes = mode_steps(place, m_bufs, m_sems, scale, eig_pair)
    next(of_modes)
    fold(paired(learning_rate * rest), 0, True)
    next(of_modes)
    for spot in place.senders():
        point_form(0, k, spot)
    next(of_points[1])
    next(of_modes)
    for spot in place.senders():
        point_form(1, k, spot)
    next(of_points[0], None)
    for spot in range(xs):
        point_form(0, 1 - k, spot)
    next(of_points[1], None)
    for spot in range(xs):
        point_form(1, 1 - k, spot)
    next(of_modes, None)
    spread(place, m_bufs[6], by_line, m_bufs[5], spread_sems, use)


def local(xs, cs, centres, weights, targets, batch_index, nystrom_index, eigvecs, mode_scale):
    rows, width = centres.shape
    batch, outs = targets.shape
    points = nystrom_index.shape[0]
    block, modes = eigvecs.shape
    deep = depth_of(width)
    total = batch + points
    mode_share = -(-(outs // 8 * block // 128) // cs)
    piece = (mode_share, 8, 128)
    sems = [1] * 2 * (4 + 4 + 3 + 7 * HALVES)
    sems = sems + [cs - 1, 1, HALVES, 1, HALVES, 1, HALVES, 1, 7]
    arrays = [
        centres.T,
        weights.T,
        targets.T,
        batch_index[None, :],
        nystrom_index[None, :],
        mode_scale[None, :],
        eigvecs,
    ]
    residual, step = pl.pallas_call(
        functools.partial(main_body, xs, cs, batch, points),
        out_shape=[pltpu.VMEM((outs, batch), F32), pltpu.VMEM((outs, rows), F32)],
        in_specs=[pl.BlockSpec(memory_space=pl.ANY)] * 7,
        out_specs=[VMEM] * 2,
        scratch_shapes=everywhere_shapes(width // 8 * batch // 128, xs, cs)
        + everywhere_shapes(outs // 8 * batch // 128, xs, cs)
        + [
            pltpu.VMEM((outs, modes), F32),
            pltpu.VMEM((1, outs, modes), F32),
            pltpu.VMEM((outs, modes), F32),
            pltpu.VMEM((xs - 1, outs, modes), F32),
            pltpu.VMEM((cs,) + piece, F32),
            pltpu.VMEM((cs - 1,) + piece, F32),
            pltpu.VMEM((CORES, xs, cs) + piece, F32),
        ]
        + point_shapes(width // 8 * points // HALVES // 128, xs, cs) * HALVES
        + [
            pltpu.VMEM((3 * width, rows), BF16),
            pltpu.VMEM((rows, deep), BF16),
            pltpu.VMEM((deep, batch), BF16),
            pltpu.VMEM((batch, deep), BF16),
            pltpu.VMEM((batch, block), BF16),
            pltpu.VMEM((batch, block), BF16),
            pltpu.VMEM((2 * outs, rows), BF16),
            pltpu.VMEM((outs, batch), F32),
            pltpu.VMEM((deep, rows), BF16),
            pltpu.VMEM((total, rows), BF16),
            pltpu.VMEM((total, rows), BF16),
        ]
        + [pltpu.SemaphoreType.DMA((n,)) for n in sems]
        + [pltpu.VMEM((xs - 1, cs) + piece, F32)]
        + [pltpu.VMEM(array.shape, array.dtype) for array in arrays]
        + [pltpu.VMEM((2, block, modes), BF16)],
        compiler_params=pltpu.CompilerParams(
            collective_id=0, has_side_effects=True, vmem_limit_bytes=65_500_000
        ),
    )(*arrays)
    return (residual.T, step.T)


def solution(mesh):
    in_specs = (
        P(("row", "col"), None),
        P(("row", "col"), None),
        P(),
        P(),
        P(),
        P("row", "col"),
        P("col"),
    )
    out_specs = (P(), P(("row", "col"), None))
    body = functools.partial(local, mesh.shape["row"] // CORES, mesh.shape["col"])
    return jax.shard_map(body, mesh=mesh, in_specs=in_specs, out_specs=out_specs, check_vma=False)
```

```python
import functools
import math

import jax
import jax.numpy as jnp
from jax import lax
from jax.experimental import pallas as pl
from jax.experimental.pallas import tpu as pltpu
from jax.sharding import PartitionSpec as P

learning_rate = 0.25
CORES = 2
HALVES = 2
MESH = pl.DeviceIdType.MESH
VMEM = pl.BlockSpec(memory_space=pltpu.VMEM)
BF16 = jnp.bfloat16
F32 = jnp.float32


def pieces(value, count):
    parts = []
    for step in range(count):
        part = value.astype(BF16).astype(F32)
        parts.append(part)
        value = value - part
    return parts


def paired(value):
    return jnp.concatenate(pieces(value, 2), axis=0).astype(BF16)


def augmented(feats, left):
    width, count = feats.shape
    unit = math.log2(math.e) / width
    square = pieces(-unit * jnp.sum(feats * feats, axis=0, keepdims=True), 3)
    if left:
        high, low = pieces(feats * (2.0 * unit), 2)
        parts, first, one = [high, low, high], 0, 3
    else:
        high, low = pieces(feats, 2)
        parts, first, one = [high, high, low], 3, 0
    spot = lax.broadcasted_iota(jnp.int32, (8, count), 0)
    tail = jnp.where((spot >= one) & (spot < one + 3), 1.0, 0.0)
    for at, part in enumerate(square):
        tail = jnp.where(spot == first + at, part, tail)
    deep = depth_of(width)
    fill = jnp.zeros((deep - 3 * width - 8, count), F32)
    return jnp.concatenate(parts + [tail, fill], axis=0)


def apply(value, eig_ref, how):
    count = value.shape[0]
    both = paired(value)
    wide = lax.dot_general(both, eig_ref[0], how, preferred_element_type=F32)
    slim = lax.dot_general(both[:count], eig_ref[1], how, preferred_element_type=F32)
    return wide[:count] + (wide[count:] + slim)


def depth_of(width):
    return -(-(3 * width + 8) // 128) * 128


def largest(count, limit):
    return max(d for d in range(1, limit + 1) if count % d == 0)


def kmul(a_ref, b_ref, w_ref, o_ref):
    points, outs = a_ref.shape[0], o_ref.shape[0]
    wide = b_ref.shape[1]
    sub = min(512, points)
    parts = largest(points // sub, 3)
    tile = min(512, wide)

    def across(i, unused):
        to = pl.ds(pl.multiple_of(i * tile, tile), tile)
        b = b_ref[:, to]

        def down(j, total):
            for part in range(parts):
                at = pl.ds(pl.multiple_of((j * parts + part) * sub, sub), sub)
                value = jnp.exp2(jnp.dot(a_ref[at, :], b, preferred_element_type=F32))
                high = value.astype(BF16)
                low = (value - high.astype(F32)).astype(BF16)
                w = w_ref[:, at]
                total = total + (
                    jnp.dot(w, high, preferred_element_type=F32)
                    + jnp.dot(w, low, preferred_element_type=F32)
                )
            return total

        total = lax.fori_loop(0, points // (sub * parts), down, jnp.zeros((2 * outs, tile), F32), unroll=True)
        o_ref[:, to] = total[:outs] + total[outs:]
        return unused

    lax.fori_loop(0, wide // tile, across, 0, unroll=True)


def split_of(xs, cs):
    ys = xs if cs % xs == 0 else 1
    return ys, cs // ys


class Place:
    def __init__(self, xs, cs):
        self.xs, self.cs = xs, cs
        self.ys, self.zs = split_of(xs, cs)
        row = lax.axis_index("row")
        self.c = lax.axis_index("col")
        self.k = lax.rem(row, CORES)
        self.x = row // CORES
        self.z, self.y = self.c // self.ys, lax.rem(self.c, self.ys)

    def device(self, k, x, c):
        return (x * CORES + k, c)

    def core(self):
        return [(1 - self.k, self.device(1 - self.k, self.x, self.c))]

    def line(self):
        spots = [lax.rem(self.x + d, self.xs) for d in range(1, self.xs)]
        return [(s, self.device(self.k, s, self.c)) for s in spots]

    def row(self):
        found = []
        for d in range(1, self.xs * CORES):
            x, k = lax.rem(self.x + d // CORES, self.xs), lax.rem(self.k + d % CORES, CORES)
            found.append(((k, x), self.device(k, x, self.c)))
        return found[::-1]

    def senders(self):
        return [lax.rem(self.x + self.xs - d, self.xs) for d in range(1, self.xs)]

    def cols(self):
        spots = [self.c ^ d for d in range(1, self.cs)]
        return [(s, self.device(self.k, self.x, s)) for s in spots]

    def plane(self):
        found = []
        for d in range(1, self.xs * self.ys):
            x = lax.rem(self.x + d // self.ys, self.xs)
            y = lax.rem(self.y + d % self.ys, self.ys)
            found.append(((x, y), self.device(self.k, x, self.z * self.ys + y)))
        return found[::-1]

    def across(self):
        spots = [lax.rem(self.y + d, self.ys) for d in range(1, self.ys)]
        return [(s, self.device(self.k, self.x, self.z * self.ys + s)) for s in spots]

    def along(self):
        spots = [lax.rem(self.z + d, self.zs) for d in range(1, self.zs)]
        return [(s, self.device(self.k, self.x, s * self.ys + self.y)) for s in spots]

    def chips(self):
        found = []
        for d in range(1, self.xs * self.cs):
            x, c = lax.rem(self.x + d // self.cs, self.xs), self.c ^ (d % self.cs)
            found.append(((x, c), self.device(self.k, x, c)))
        return found[::-1]

    def arrive(self):
        sem = pltpu.get_barrier_semaphore()
        everyone = self.core() + self.chips()
        for spot, device in everyone:
            pl.semaphore_signal(sem, inc=1, device_id=device, device_id_type=MESH)
        return lambda: pl.semaphore_wait(sem, len(everyone))


def start(partners, source, target, sems):
    copies = []
    for d, (spot, device) in enumerate(partners):
        copies.append(
            pltpu.make_async_remote_copy(
                src_ref=source(d, spot),
                dst_ref=target(d, spot),
                send_sem=sems[0],
                recv_sem=sems[1],
                device_id=device,
                device_id_type=MESH,
            )
        )
    for copy in copies:
        copy.start()
    return copies


def await_all(whole, sem):
    pltpu.make_async_copy(whole, whole, sem).wait()


def finish(whole, sems):
    for sem in sems:
        await_all(whole, sem)


def summed(first, buffers, count):
    total = first
    for d in range(count):
        total = total + buffers[d]
    return total


def everywhere_steps(place, bufs, sems):
    in_ref, by_core, on_core, by_chip, o_ref = bufs
    k, x, c = place.k, place.x, place.c
    start(place.core(), lambda d, s: in_ref.at[s], lambda d, s: by_core.at[d], sems[0])
    yield
    finish(by_core, sems[0])
    on_core[...] = in_ref[k] + by_core[0]
    start(place.chips(), lambda d, s: on_core.at[s], lambda d, s: by_chip.at[d], sems[1])
    yield
    finish(by_chip, sems[1])
    o_ref[k, x, c] = summed(on_core[x, c], by_chip, by_chip.shape[0])
    start(
        place.chips(), lambda d, s: o_ref.at[k, x, c], lambda d, s: o_ref.at[k, x, c], sems[2]
    )
    yield
    finish(by_chip, sems[2])
    start(place.core(), lambda d, s: o_ref.at[k], lambda d, s: o_ref.at[k], sems[3])
    yield
    finish(by_core, sems[3])


def point_steps(place, bufs, sems):
    in_ref, by_core, on_core, by_plane, on_plane, by_line, o_ref = bufs
    k, x, y, z = place.k, place.x, place.y, place.z
    start(place.core(), lambda d, s: in_ref.at[s], lambda d, s: by_core.at[d], sems[0])
    yield
    finish(by_core, sems[0])
    on_core[...] = in_ref[k] + by_core[0]
    start(place.plane(), lambda d, s: on_core.at[s], lambda d, s: by_plane.at[d], sems[1])
    yield
    finish(by_plane, sems[1])
    on_plane[...] = summed(on_core[x, y], by_plane, by_plane.shape[0])
    start(place.along(), lambda d, s: on_plane.at[s], lambda d, s: by_line.at[d], sems[2])
    yield
    finish(by_line, sems[2])
    o_ref[k, x, y, z] = summed(on_plane[z], by_line, place.zs - 1)
    piece = lambda d, s: o_ref.at[k, x, y, z]
    start(place.along(), piece, piece, sems[3])
    yield
    finish(by_line, sems[3])
    piece = lambda d, s: o_ref.at[k, x, y]
    start(place.across(), piece, piece, sems[4])
    yield
    finish(by_plane.at[pl.ds(0, place.ys - 1)], sems[4])
    piece = lambda d, s: o_ref.at[k, x]
    start(place.line(), piece, piece, sems[5])
    yield
    finish(on_core.at[pl.ds(0, place.xs - 1)], sems[5])
    piece = lambda d, s: o_ref.at[k]
    start(place.core(), piece, piece, sems[6])
    yield
    finish(by_core, sems[6])


def mode_steps(place, bufs, sems, scale_ref, eig_ref):
    part, by_row, terms, by_col, o_ref = bufs
    start(place.row(), lambda d, s: part, lambda d, s: by_row.at[d], sems[0])
    yield
    finish(by_row, sems[0])
    coeff = summed(part[...], by_row, by_row.shape[0]) * scale_ref[...]
    correction = apply(coeff, eig_ref, (((1,), (1,)), ((), ())))
    store_tiles(correction, 0, lambda t, tile: place_in(terms, t, tile))
    start(place.cols(), lambda d, s: terms.at[s], lambda d, s: by_col.at[d], sems[1])
    yield
    finish(by_col, sems[1])
    o_ref[place.k, place.x, place.c] = summed(terms[place.c], by_col, place.cs - 1)


def spread(place, o_ref, by_line, by_col, sems, use):
    k, x, c, cs = place.k, place.x, place.c, place.cs
    size = cs // HALVES
    own, own_sent, line, line_sent, near, near_sent, far, far_sent = sems
    halves = [c // size, 1 - c // size]
    part = lambda ref, at: ref.at[pl.ds(at * size, size)]

    def across(d):
        piece = lambda e, s: o_ref.at[k, x, c ^ d]
        start(place.line(), piece, piece, [line_sent.at[0], line.at[d // size]])

    def beside(ref, at, ends):
        piece = lambda d, s: part(ref, at)
        start(place.core(), piece, piece, ends)

    mine = [
        start([partner], lambda d, s: o_ref.at[k, x, c], lambda d, s: o_ref.at[k, x, c], [own_sent.at[0], own.at[d]])
        for d, partner in enumerate(place.cols())
    ]
    across(0)
    for h in range(HALVES):
        for d in range(max(1, h * size), (h + 1) * size):
            await_all(o_ref.at[k, x, c], own.at[d - 1])
            across(d)
        beside(o_ref.at[k, x], halves[h], [near_sent.at[0], near.at[h]])
        use(k, x, halves[h])
    for h in range(HALVES):
        await_all(part(o_ref.at[k, x], 0), near.at[h])
        use(1 - k, x, halves[h])
    for h in range(HALVES):
        await_all(by_line.at[:, pl.ds(0, size)], line.at[h])
        for spot in place.senders():
            beside(o_ref.at[k, spot], halves[h], [far_sent.at[0], far.at[h]])
        for spot in place.senders():
            use(k, spot, halves[h])
        await_all(by_line.at[:, pl.ds(0, size)], far.at[h])
        for spot in place.senders():
            use(1 - k, spot, halves[h])
    await_all(by_col, own_sent.at[0])
    await_all(by_line, line_sent.at[0])
    await_all(o_ref.at[k, x], near_sent.at[0])
    await_all(by_line, far_sent.at[0])


def spot_in(shape, t):
    spots = []
    for count in reversed(shape):
        t, spot = divmod(t, count)
        spots.append(spot)
    return t, tuple(reversed(spots))


def spot_of(shape, t):
    row, spots = spot_in(shape[2:-2], t)
    return (row % CORES, row // CORES) + spots


def place_in(terms, t, tile):
    terms[divmod(t, terms.shape[1])] = tile


def store_tiles(value, block, put):
    high = value.shape[0] // 8
    for j in range(value.shape[1] // 128):
        for g in range(high):
            put((block + j) * high + g, value[8 * g : 8 * g + 8, 128 * j : 128 * j + 128])


def store_all(buf, block, value):
    def put(t, tile):
        buf[spot_of(buf.shape, t)] = tile

    store_tiles(value, block, put)


def load_tiles(get, high, block, blocks):
    columns = []
    for j in range(block, block + blocks):
        columns.append(jnp.concatenate([get(j * high + g) for g in range(high)], axis=0))
    return jnp.concatenate(columns, axis=1) if blocks > 1 else columns[0]


def load_all(buf, high, block, blocks):
    return load_tiles(lambda t: buf[spot_of(buf.shape, t)], high, block, blocks)


def share_of(tiles, xs, cs):
    return -(-tiles // (CORES * xs * cs))


def everywhere_shapes(tiles, xs, cs):
    piece = (share_of(tiles, xs, cs), 8, 128)
    shapes = [
        (CORES, xs, cs) + piece,
        (1, xs, cs) + piece,
        (xs, cs) + piece,
        (xs * cs - 1,) + piece,
        (CORES, xs, cs) + piece,
    ]
    return [pltpu.VMEM(shape, F32) for shape in shapes]


def point_shapes(tiles, xs, cs):
    piece = (share_of(tiles, xs, cs), 8, 128)
    ys, zs = split_of(xs, cs)
    shapes = [
        (CORES, xs, ys, zs) + piece,
        (1, xs, ys, zs) + piece,
        (xs, ys, zs) + piece,
        (xs * ys - 1, zs) + piece,
        (zs,) + piece,
        (zs - 1,) + piece,
        (CORES, xs, ys, zs) + piece,
    ]
    return [pltpu.VMEM(shape, F32) for shape in shapes]


CHUNK = 512


def main_body(
    xs, cs, batch, points, centres_in, weights_in, targets_in, batch_in, points_in, scale_in, eig_in,
    residual, step, *scratch
):
    width, rows = centres_in.shape
    outs = targets_in.shape[0]
    block = eig_in.shape[0]
    some = block // HALVES
    high = width // 8
    scratch = list(scratch)
    take = lambda count: [scratch.pop(0) for i in range(count)]
    pair = lambda count: [[ref.at[0] for ref in take(2)] for i in range(count)]
    b_bufs, p_bufs, m_bufs = take(5), take(5), take(5)
    n_bufs = [take(7) for h in range(HALVES)]
    split, left_rows, batch_right, batch_left, block_high, block_low, pairs, pred = take(8)
    left, kern_high, kern_low = take(3)
    b_sems, p_sems, m_sems = pair(4), pair(4), pair(2)
    n_sems = [pair(7) for h in range(HALVES)]
    spread_sems, input_sems = take(8), take(1)[0]
    by_line = take(1)[0]
    inputs = take(7)
    eig_pair = take(1)[0]
    place = Place(xs, cs)
    k, x, c = place.k, place.x, place.c
    met = place.arrive()
    sources = [centres_in, weights_in, targets_in, batch_in, points_in, scale_in, eig_in]
    loads = [
        pltpu.make_async_copy(source, ref, input_sems.at[i])
        for i, (source, ref) in enumerate(zip(sources, inputs))
    ]
    for i in (0, 3, 4, 1, 2, 5, 6):
        loads[i].start()
    centres, weights, targets, batch_at, points_at, scale, eig = inputs
    offset = lax.axis_index(("row", "col")) * rows

    def pick(index):
        count = index.shape[1]
        spot = lax.broadcasted_iota(jnp.int32, (rows, count), 0)
        hot = jnp.where(spot == index - offset, 1.0, 0.0).astype(BF16)
        got = jnp.dot(split[...], hot, preferred_element_type=F32)
        return (got[:width] + got[width : 2 * width]) + got[2 * width :]

    def pick_points(h, first, last):
        groups = points // block
        for row in range(first * groups // 2, last * groups // 2):
            at = row * block + h * some
            store_all(n_bufs[h][0], row * some // 128, pick(points_at[:, at : at + some]))

    def keep_kernel(first, points_rows):
        count = points_rows.shape[0]
        tile = min(CHUNK, rows)

        def across(i, unused):
            to = pl.ds(pl.multiple_of(i * tile, tile), tile)
            value = jnp.exp2(jnp.dot(points_rows, left[:, to], preferred_element_type=F32))
            near = value.astype(BF16)
            kern_high[pl.ds(first, count), to] = near
            kern_low[pl.ds(first, count), to] = (value - near.astype(F32)).astype(BF16)
            return unused

        lax.fori_loop(0, rows // tile, across, 0, unroll=True)

    def fold(w, first, begin):
        tile = min(CHUNK, rows)
        rest = pl.ds(first, w.shape[1])

        def across(i, unused):
            to = pl.ds(pl.multiple_of(i * tile, tile), tile)
            total = jnp.dot(w, kern_high[rest, to], preferred_element_type=F32)
            total = total + jnp.dot(w, kern_low[rest, to], preferred_element_type=F32)
            total = total[:outs] + total[outs:]
            step[:, to] = total if begin else step[:, to] + total
            return unused

        lax.fori_loop(0, rows // tile, across, 0, unroll=True)

    def row_at(k, x, h):
        return batch + pl.multiple_of((x * CORES + k) * block + h * some, some)

    def feats_of(h, k, x):
        mine = n_bufs[h][6].at[k, x]
        return load_tiles(lambda t: mine[spot_in(mine.shape[:-2], t)[1]], high, 0, some // 128)

    def point_form(h, k, x):
        keep_kernel(row_at(k, x, h), augmented(feats_of(h, k, x), False).T.astype(BF16))

    def own_form(h):
        form = augmented(feats_of(h, k, x), False)
        to = slice(h * some, h * some + some)
        value = jnp.exp2(jnp.dot(batch_left[...], form.astype(BF16), preferred_element_type=F32))
        near = value.astype(BF16)
        block_high[:, to] = near
        block_low[:, to] = (value - near.astype(F32)).astype(BF16)

    def use(k, x, h):
        size = cs // HALVES
        mine = m_bufs[4].at[k, x, pl.ds(h * size, size)]
        correction = load_tiles(lambda t: mine[divmod(t, mine.shape[1])], outs // 8, 0, some // 128)
        fold(paired(-learning_rate * correction), row_at(k, x, h), False)

    for bufs in [b_bufs, p_bufs] + n_bufs:
        bufs[0][...] = jnp.zeros_like(bufs[0])
    loads[0].wait()
    loads[3].wait()
    split[...] = jnp.concatenate(pieces(centres[...], 3), axis=0).astype(BF16)
    for at in range(0, batch, CHUNK):
        store_all(b_bufs[0], at // 128, pick(batch_at[:, at : min(at + CHUNK, batch)]))
    loads[4].wait()
    met()
    of_batch = everywhere_steps(place, b_bufs, b_sems)
    of_pred = everywhere_steps(place, p_bufs, p_sems)
    of_points = [point_steps(place, n_bufs[h], n_sems[h]) for h in range(HALVES)]
    next(of_batch)
    pick_points(0, 0, 1)
    next(of_batch)
    pick_points(0, 1, 2)
    next(of_points[0])
    pick_points(1, 0, 2)
    next(of_points[1])
    next(of_points[0])
    next(of_batch)
    next(of_points[1])
    for at in range(0, rows, CHUNK):
        to = slice(at, min(at + CHUNK, rows))
        form = augmented(centres[:, to], True)
        left[:, to] = form.astype(BF16)
        left_rows[to, :] = form.T.astype(BF16)
    for i in (1, 2, 5, 6):
        loads[i].wait()
    pairs[...] = paired(weights[...])
    eig_pair[0], eig_pair[1] = [part.astype(BF16) for part in pieces(eig[...], 2)]
    next(of_points[0])
    next(of_batch)
    next(of_points[1])
    next(of_batch, None)

    feats = load_all(b_bufs[4], high, 0, batch // 128)
    form = augmented(feats, False)
    batch_right[...] = form.astype(BF16)
    kmul(left_rows, batch_right, pairs, pred)
    store_all(p_bufs[0], 0, pred[...])
    next(of_pred)
    next(of_points[0])
    batch_left[...] = augmented(feats, True).T.astype(BF16)
    next(of_pred)
    next(of_points[1])
    keep_kernel(0, form.T.astype(BF16))
    next(of_points[0])
    next(of_pred)
    next(of_points[1])
    next(of_points[0])
    own_form(0)
    point_form(0, k, x)
    next(of_points[1])
    own_form(1)
    next(of_pred)
    point_form(1, k, x)
    next(of_pred, None)

    rest = load_all(p_bufs[4], outs // 8, 0, batch // 128) - targets[...]
    residual[...] = rest
    pair_rest = paired(rest)
    grad = jnp.dot(pair_rest, block_high[...], preferred_element_type=F32)
    grad = grad + jnp.dot(pair_rest, block_low[...], preferred_element_type=F32)
    m_bufs[0][...] = apply(grad[:outs] + grad[outs:], eig_pair, (((1,), (0,)), ((), ())))
    of_modes = mode_steps(place, m_bufs, m_sems, scale, eig_pair)
    next(of_modes)
    next(of_points[0])
    fold(paired(learning_rate * rest), 0, True)
    for spot in place.senders():
        point_form(0, k, spot)
    next(of_points[1])
    next(of_modes)
    for spot in place.senders():
        point_form(1, k, spot)
    next(of_points[0], None)
    for spot in range(xs):
        point_form(0, 1 - k, spot)
    next(of_points[1], None)
    for spot in range(xs):
        point_form(1, 1 - k, spot)
    next(of_modes, None)
    spread(place, m_bufs[4], by_line, m_bufs[3], spread_sems, use)


def local(xs, cs, centres, weights, targets, batch_index, nystrom_index, eigvecs, mode_scale):
    rows, width = centres.shape
    batch, outs = targets.shape
    points = nystrom_index.shape[0]
    block, modes = eigvecs.shape
    deep = depth_of(width)
    total = batch + points
    mode_share = -(-(outs // 8 * block // 128) // cs)
    piece = (mode_share, 8, 128)
    sems = [1] * 2 * (4 + 4 + 2 + 7 * HALVES)
    sems = sems + [cs - 1, 1, HALVES, 1, HALVES, 1, HALVES, 1, 7]
    arrays = [
        centres.T,
        weights.T,
        targets.T,
        batch_index[None, :],
        nystrom_index[None, :],
        mode_scale[None, :],
        eigvecs,
    ]
    residual, step = pl.pallas_call(
        functools.partial(main_body, xs, cs, batch, points),
        out_shape=[pltpu.VMEM((outs, batch), F32), pltpu.VMEM((outs, rows), F32)],
        in_specs=[pl.BlockSpec(memory_space=pl.ANY)] * 7,
        out_specs=[VMEM] * 2,
        scratch_shapes=everywhere_shapes(width // 8 * batch // 128, xs, cs)
        + everywhere_shapes(outs // 8 * batch // 128, xs, cs)
        + [
            pltpu.VMEM((outs, modes), F32),
            pltpu.VMEM((CORES * xs - 1, outs, modes), F32),
            pltpu.VMEM((cs,) + piece, F32),
            pltpu.VMEM((cs - 1,) + piece, F32),
            pltpu.VMEM((CORES, xs, cs) + piece, F32),
        ]
        + point_shapes(width // 8 * points // HALVES // 128, xs, cs) * HALVES
        + [
            pltpu.VMEM((3 * width, rows), BF16),
            pltpu.VMEM((rows, deep), BF16),
            pltpu.VMEM((deep, batch), BF16),
            pltpu.VMEM((batch, deep), BF16),
            pltpu.VMEM((batch, block), BF16),
            pltpu.VMEM((batch, block), BF16),
            pltpu.VMEM((2 * outs, rows), BF16),
            pltpu.VMEM((outs, batch), F32),
            pltpu.VMEM((deep, rows), BF16),
            pltpu.VMEM((total, rows), BF16),
            pltpu.VMEM((total, rows), BF16),
        ]
        + [pltpu.SemaphoreType.DMA((n,)) for n in sems]
        + [pltpu.VMEM((xs - 1, cs) + piece, F32)]
        + [pltpu.VMEM(array.shape, array.dtype) for array in arrays]
        + [pltpu.VMEM((2, block, modes), BF16)],
        compiler_params=pltpu.CompilerParams(
            collective_id=0, has_side_effects=True, vmem_limit_bytes=65_500_000
        ),
    )(*arrays)
    return (residual.T, step.T)


def solution(mesh):
    in_specs = (
        P(("row", "col"), None),
        P(("row", "col"), None),
        P(),
        P(),
        P(),
        P("row", "col"),
        P("col"),
    )
    out_specs = (P(), P(("row", "col"), None))
    body = functools.partial(local, mesh.shape["row"] // CORES, mesh.shape["col"])
    return jax.shard_map(body, mesh=mesh, in_specs=in_specs, out_specs=out_specs, check_vma=False)
```

```python
import functools
import math

import jax
import jax.numpy as jnp
from jax import lax
from jax.experimental import pallas as pl
from jax.experimental.pallas import tpu as pltpu
from jax.sharding import PartitionSpec as P

learning_rate = 0.25
CORES = 2
HALVES = 2
MESH = pl.DeviceIdType.MESH
VMEM = pl.BlockSpec(memory_space=pltpu.VMEM)
BF16 = jnp.bfloat16
F32 = jnp.float32


def pieces(value, count):
    parts = []
    for step in range(count):
        part = value.astype(BF16).astype(F32)
        parts.append(part)
        value = value - part
    return parts


def paired(value):
    return jnp.concatenate(pieces(value, 2), axis=0).astype(BF16)


def augmented(feats, left):
    width, count = feats.shape
    unit = math.log2(math.e) / width
    square = pieces(-unit * jnp.sum(feats * feats, axis=0, keepdims=True), 3)
    if left:
        high, low = pieces(feats * (2.0 * unit), 2)
        parts, first, one = [high, low, high], 0, 3
    else:
        high, low = pieces(feats, 2)
        parts, first, one = [high, high, low], 3, 0
    spot = lax.broadcasted_iota(jnp.int32, (8, count), 0)
    tail = jnp.where((spot >= one) & (spot < one + 3), 1.0, 0.0)
    for at, part in enumerate(square):
        tail = jnp.where(spot == first + at, part, tail)
    deep = depth_of(width)
    fill = jnp.zeros((deep - 3 * width - 8, count), F32)
    return jnp.concatenate(parts + [tail, fill], axis=0)


def apply(value, eig_ref, how):
    count = value.shape[0]
    both = paired(value)
    wide = lax.dot_general(both, eig_ref[0], how, preferred_element_type=F32)
    slim = lax.dot_general(both[:count], eig_ref[1], how, preferred_element_type=F32)
    return wide[:count] + (wide[count:] + slim)


def depth_of(width):
    return -(-(3 * width + 8) // 128) * 128


def largest(count, limit):
    return max(d for d in range(1, limit + 1) if count % d == 0)


def kmul(a_ref, b, w_ref):
    points, outs = a_ref.shape[0], w_ref.shape[0] // 2
    sub = min(512, points)
    total = jnp.zeros((2 * outs, b.shape[1]), F32)
    for part in range(points // sub):
        at = slice(part * sub, part * sub + sub)
        value = jnp.exp2(jnp.dot(a_ref[at, :], b, preferred_element_type=F32))
        high = value.astype(BF16)
        low = (value - high.astype(F32)).astype(BF16)
        w = w_ref[:, at]
        total = total + (
            jnp.dot(w, high, preferred_element_type=F32)
            + jnp.dot(w, low, preferred_element_type=F32)
        )
    return total[:outs] + total[outs:]


def split_of(xs, cs):
    ys = xs if cs % xs == 0 else 1
    return ys, cs // ys


class Place:
    def __init__(self, xs, cs):
        self.xs, self.cs = xs, cs
        self.ys, self.zs = split_of(xs, cs)
        row = lax.axis_index("row")
        self.c = lax.axis_index("col")
        self.k = lax.rem(row, CORES)
        self.x = row // CORES
        self.z, self.y = self.c // self.ys, lax.rem(self.c, self.ys)

    def device(self, k, x, c):
        return (x * CORES + k, c)

    def core(self):
        return [(1 - self.k, self.device(1 - self.k, self.x, self.c))]

    def line(self):
        spots = [lax.rem(self.x + d, self.xs) for d in range(1, self.xs)]
        return [(s, self.device(self.k, s, self.c)) for s in spots]

    def row(self):
        found = []
        for d in range(1, self.xs * CORES):
            x, k = lax.rem(self.x + d // CORES, self.xs), lax.rem(self.k + d % CORES, CORES)
            found.append(((k, x), self.device(k, x, self.c)))
        return found[::-1]

    def senders(self):
        return [lax.rem(self.x + self.xs - d, self.xs) for d in range(1, self.xs)]

    def cols(self):
        spots = [self.c ^ d for d in range(1, self.cs)]
        return [(s, self.device(self.k, self.x, s)) for s in spots]

    def plane(self):
        found = []
        for d in range(1, self.xs * self.ys):
            x = lax.rem(self.x + d // self.ys, self.xs)
            y = lax.rem(self.y + d % self.ys, self.ys)
            found.append(((x, y), self.device(self.k, x, self.z * self.ys + y)))
        return found[::-1]

    def across(self):
        spots = [lax.rem(self.y + d, self.ys) for d in range(1, self.ys)]
        return [(s, self.device(self.k, self.x, self.z * self.ys + s)) for s in spots]

    def along(self):
        spots = [lax.rem(self.z + d, self.zs) for d in range(1, self.zs)]
        return [(s, self.device(self.k, self.x, s * self.ys + self.y)) for s in spots]

    def chips(self):
        found = []
        for d in range(1, self.xs * self.cs):
            x, c = lax.rem(self.x + d // self.cs, self.xs), self.c ^ (d % self.cs)
            found.append(((x, c), self.device(self.k, x, c)))
        return found[::-1]

    def arrive(self):
        sem = pltpu.get_barrier_semaphore()
        everyone = self.core() + self.chips()
        for spot, device in everyone:
            pl.semaphore_signal(sem, inc=1, device_id=device, device_id_type=MESH)
        return lambda: pl.semaphore_wait(sem, len(everyone))


def start(partners, source, target, sems):
    copies = []
    for d, (spot, device) in enumerate(partners):
        copies.append(
            pltpu.make_async_remote_copy(
                src_ref=source(d, spot),
                dst_ref=target(d, spot),
                send_sem=sems[0],
                recv_sem=sems[1],
                device_id=device,
                device_id_type=MESH,
            )
        )
    for copy in copies:
        copy.start()
    return copies


def await_all(whole, sem):
    pltpu.make_async_copy(whole, whole, sem).wait()


def finish(whole, sems):
    for sem in sems:
        await_all(whole, sem)


def summed(first, buffers, count):
    total = first
    for d in range(count):
        total = total + buffers[d]
    return total


def everywhere_steps(place, bufs, sems):
    in_ref, by_core, on_core, by_chip, o_ref = bufs
    k, x, c = place.k, place.x, place.c
    start(place.core(), lambda d, s: in_ref.at[s], lambda d, s: by_core.at[d], sems[0])
    yield
    finish(by_core, sems[0])
    on_core[...] = in_ref[k] + by_core[0]
    start(place.chips(), lambda d, s: on_core.at[s], lambda d, s: by_chip.at[d], sems[1])
    yield
    finish(by_chip, sems[1])
    o_ref[k, x, c] = summed(on_core[x, c], by_chip, by_chip.shape[0])
    start(
        place.chips(), lambda d, s: o_ref.at[k, x, c], lambda d, s: o_ref.at[k, x, c], sems[2]
    )
    yield
    finish(by_chip, sems[2])
    start(place.core(), lambda d, s: o_ref.at[k], lambda d, s: o_ref.at[k], sems[3])
    yield
    finish(by_core, sems[3])


def point_steps(place, bufs, sems):
    in_ref, by_core, on_core, by_plane, on_plane, by_line, o_ref = bufs
    k, x, y, z = place.k, place.x, place.y, place.z
    start(place.core(), lambda d, s: in_ref.at[s], lambda d, s: by_core.at[d], sems[0])
    yield
    finish(by_core, sems[0])
    on_core[...] = in_ref[k] + by_core[0]
    start(place.plane(), lambda d, s: on_core.at[s], lambda d, s: by_plane.at[d], sems[1])
    yield
    finish(by_plane, sems[1])
    on_plane[...] = summed(on_core[x, y], by_plane, by_plane.shape[0])
    start(place.along(), lambda d, s: on_plane.at[s], lambda d, s: by_line.at[d], sems[2])
    yield
    finish(by_line, sems[2])
    o_ref[k, x, y, z] = summed(on_plane[z], by_line, place.zs - 1)
    piece = lambda d, s: o_ref.at[k, x, y, z]
    start(place.along(), piece, piece, sems[3])
    yield
    finish(by_line, sems[3])
    piece = lambda d, s: o_ref.at[k, x, y]
    start(place.across(), piece, piece, sems[4])
    yield
    finish(by_plane.at[pl.ds(0, place.ys - 1)], sems[4])
    piece = lambda d, s: o_ref.at[k, x]
    start(place.line(), piece, piece, sems[5])
    yield
    finish(on_core.at[pl.ds(0, place.xs - 1)], sems[5])
    piece = lambda d, s: o_ref.at[k]
    start(place.core(), piece, piece, sems[6])
    yield
    finish(by_core, sems[6])


def mode_steps(place, bufs, sems, scale_ref, eig_ref):
    part, by_row, terms, by_col, o_ref = bufs
    start(place.row(), lambda d, s: part, lambda d, s: by_row.at[d], sems[0])
    yield
    finish(by_row, sems[0])
    coeff = summed(part[...], by_row, by_row.shape[0]) * scale_ref[...]
    correction = apply(coeff, eig_ref, (((1,), (0,)), ((), ())))
    store_tiles(correction, 0, lambda t, tile: place_in(terms, t, tile))
    start(place.cols(), lambda d, s: terms.at[s], lambda d, s: by_col.at[d], sems[1])
    yield
    finish(by_col, sems[1])
    o_ref[place.k, place.x, place.c] = summed(terms[place.c], by_col, place.cs - 1)


def spread(place, o_ref, by_line, by_col, sems, use):
    k, x, c, cs = place.k, place.x, place.c, place.cs
    size = cs // HALVES
    own, own_sent, line, line_sent, near, near_sent, far, far_sent = sems
    halves = [c // size, 1 - c // size]
    part = lambda ref, at: ref.at[pl.ds(at * size, size)]

    def across(d):
        piece = lambda e, s: o_ref.at[k, x, c ^ d]
        start(place.line(), piece, piece, [line_sent.at[0], line.at[d // size]])

    def beside(ref, at, ends):
        piece = lambda d, s: part(ref, at)
        start(place.core(), piece, piece, ends)

    mine = [
        start([partner], lambda d, s: o_ref.at[k, x, c], lambda d, s: o_ref.at[k, x, c], [own_sent.at[0], own.at[d]])
        for d, partner in enumerate(place.cols())
    ]
    across(0)
    for h in range(HALVES):
        for d in range(max(1, h * size), (h + 1) * size):
            await_all(o_ref.at[k, x, c], own.at[d - 1])
            across(d)
        beside(o_ref.at[k, x], halves[h], [near_sent.at[0], near.at[h]])
        use(k, x, halves[h])
    for h in range(HALVES):
        await_all(part(o_ref.at[k, x], 0), near.at[h])
        use(1 - k, x, halves[h])
    for h in range(HALVES):
        await_all(by_line.at[:, pl.ds(0, size)], line.at[h])
        for spot in place.senders():
            beside(o_ref.at[k, spot], halves[h], [far_sent.at[0], far.at[h]])
        for spot in place.senders():
            use(k, spot, halves[h])
        await_all(by_line.at[:, pl.ds(0, size)], far.at[h])
        for spot in place.senders():
            use(1 - k, spot, halves[h])
    await_all(by_col, own_sent.at[0])
    await_all(by_line, line_sent.at[0])
    await_all(o_ref.at[k, x], near_sent.at[0])
    await_all(by_line, far_sent.at[0])


def spot_in(shape, t):
    spots = []
    for count in reversed(shape):
        t, spot = divmod(t, count)
        spots.append(spot)
    return t, tuple(reversed(spots))


def spot_of(shape, t, other=False):
    row, spots = spot_in(shape[2:-2], t)
    core = row % CORES
    return (1 - core if other else core, row // CORES) + spots


def place_in(terms, t, tile):
    terms[divmod(t, terms.shape[1])] = tile


def store_tiles(value, block, put):
    high = value.shape[0] // 8
    for j in range(value.shape[1] // 128):
        for g in range(high):
            put((block + j) * high + g, value[8 * g : 8 * g + 8, 128 * j : 128 * j + 128])


def store_all(buf, block, value, other=False):
    def put(t, tile):
        buf[spot_of(buf.shape, t, other)] = tile

    store_tiles(value, block, put)


def load_tiles(get, high, block, blocks):
    columns = []
    for j in range(block, block + blocks):
        columns.append(jnp.concatenate([get(j * high + g) for g in range(high)], axis=0))
    return jnp.concatenate(columns, axis=1) if blocks > 1 else columns[0]


def load_all(buf, high, block, blocks, other=False):
    return load_tiles(lambda t: buf[spot_of(buf.shape, t, other)], high, block, blocks)


def share_of(tiles, xs, cs):
    return -(-tiles // (CORES * xs * cs))


def everywhere_shapes(tiles, xs, cs):
    piece = (share_of(tiles, xs, cs), 8, 128)
    shapes = [
        (CORES, xs, cs) + piece,
        (1, xs, cs) + piece,
        (xs, cs) + piece,
        (xs * cs - 1,) + piece,
        (CORES, xs, cs) + piece,
    ]
    return [pltpu.VMEM(shape, F32) for shape in shapes]


def point_shapes(tiles, xs, cs):
    piece = (share_of(tiles, xs, cs), 8, 128)
    ys, zs = split_of(xs, cs)
    shapes = [
        (CORES, xs, ys, zs) + piece,
        (1, xs, ys, zs) + piece,
        (xs, ys, zs) + piece,
        (xs * ys - 1, zs) + piece,
        (zs,) + piece,
        (zs - 1,) + piece,
        (CORES, xs, ys, zs) + piece,
    ]
    return [pltpu.VMEM(shape, F32) for shape in shapes]


CHUNK = 512


def main_body(
    xs, cs, batch, points, centres_in, weights_in, targets_in, batch_in, points_in, scale_in, eig_in,
    residual, step, *scratch
):
    width, rows = centres_in.shape
    outs = targets_in.shape[0]
    block = eig_in.shape[0]
    some = block // HALVES
    high = width // 8
    tiles_of = lambda rows: cs * share_of(rows // 8 * batch // 128, xs, cs)
    by_block = batch // 128 == CORES * xs and tiles_of(width) == high and tiles_of(outs) == outs // 8
    scratch = list(scratch)
    take = lambda count: [scratch.pop(0) for i in range(count)]
    pair = lambda count: [[ref.at[0] for ref in take(2)] for i in range(count)]
    b_bufs, p_bufs, m_bufs = take(5), take(5), take(5)
    n_bufs = [take(7) for h in range(HALVES)]
    split, left_rows, batch_left, block_high, block_low, pairs = take(6)
    left, kern_high, kern_low = take(3)
    b_sems, p_sems, m_sems = pair(4), pair(4), pair(2)
    n_sems = [pair(7) for h in range(HALVES)]
    spread_sems, input_sems = take(8), take(1)[0]
    by_line = take(1)[0]
    inputs = take(7)
    eig_pair, eig_turned = take(2)
    place = Place(xs, cs)
    k, x, c = place.k, place.x, place.c
    met = place.arrive()
    sources = [centres_in, weights_in, targets_in, batch_in, points_in, scale_in, eig_in]
    loads = [
        pltpu.make_async_copy(source, ref, input_sems.at[i])
        for i, (source, ref) in enumerate(zip(sources, inputs))
    ]
    for i in (0, 3, 4, 1, 2, 5, 6):
        loads[i].start()
    centres, weights, targets, batch_at, points_at, scale, eig = inputs
    offset = lax.axis_index(("row", "col")) * rows

    def pick(index):
        count = index.shape[1]
        spot = lax.broadcasted_iota(jnp.int32, (rows, count), 0)
        hot = jnp.where(spot == index - offset, 1.0, 0.0).astype(BF16)
        got = jnp.dot(split[...], hot, preferred_element_type=F32)
        return (got[:width] + got[width : 2 * width]) + got[2 * width :]

    def pick_points(h, first, last):
        groups = points // block
        for row in range(first * groups // 2, last * groups // 2):
            at = row * block + h * some
            store_all(n_bufs[h][0], row * some // 128, pick(points_at[:, at : at + some]))

    def keep_kernel(first, points_rows):
        count = points_rows.shape[0]
        tile = min(CHUNK, rows)

        def across(i, unused):
            to = pl.ds(pl.multiple_of(i * tile, tile), tile)
            value = jnp.exp2(jnp.dot(points_rows, left[:, to], preferred_element_type=F32))
            near = value.astype(BF16)
            kern_high[pl.ds(first, count), to] = near
            kern_low[pl.ds(first, count), to] = (value - near.astype(F32)).astype(BF16)
            return unused

        lax.fori_loop(0, rows // tile, across, 0, unroll=True)

    def fold(w, first, begin):
        tile = min(CHUNK, rows)
        rest = pl.ds(first, w.shape[1])

        def across(i, unused):
            to = pl.ds(pl.multiple_of(i * tile, tile), tile)
            total = jnp.dot(w, kern_high[rest, to], preferred_element_type=F32)
            total = total + jnp.dot(w, kern_low[rest, to], preferred_element_type=F32)
            total = total[:outs] + total[outs:]
            step[:, to] = total if begin else step[:, to] + total
            return unused

        lax.fori_loop(0, rows // tile, across, 0, unroll=True)

    def row_at(k, x, h):
        return batch + pl.multiple_of((x * CORES + k) * block + h * some, some)

    def feats_of(h, k, x):
        mine = n_bufs[h][6].at[k, x]
        return load_tiles(lambda t: mine[spot_in(mine.shape[:-2], t)[1]], high, 0, some // 128)

    def point_form(h, k, x):
        keep_kernel(row_at(k, x, h), augmented(feats_of(h, k, x), False).T.astype(BF16))

    def own_form(h):
        form = augmented(feats_of(h, k, x), False)
        to = slice(h * some, h * some + some)
        value = jnp.exp2(jnp.dot(batch_left[...], form.astype(BF16), preferred_element_type=F32))
        near = value.astype(BF16)
        block_high[:, to] = near
        block_low[:, to] = (value - near.astype(F32)).astype(BF16)

    def use(k, x, h):
        size = cs // HALVES
        mine = m_bufs[4].at[k, x, pl.ds(h * size, size)]
        correction = load_tiles(lambda t: mine[divmod(t, mine.shape[1])], outs // 8, 0, some // 128)
        fold(paired(-learning_rate * correction), row_at(k, x, h), False)

    for bufs in [b_bufs, p_bufs] + n_bufs:
        bufs[0][...] = jnp.zeros_like(bufs[0])
    loads[0].wait()
    loads[3].wait()
    split[...] = jnp.concatenate(pieces(centres[...], 3), axis=0).astype(BF16)
    for at in range(0, batch, CHUNK):
        store_all(b_bufs[0], at // 128, pick(batch_at[:, at : min(at + CHUNK, batch)]))
    loads[4].wait()
    met()
    of_batch = everywhere_steps(place, b_bufs, b_sems)
    of_pred = everywhere_steps(place, p_bufs, p_sems)
    of_points = [point_steps(place, n_bufs[h], n_sems[h]) for h in range(HALVES)]
    next(of_batch)
    pick_points(0, 0, 1)
    next(of_batch)
    pick_points(0, 1, 2)
    next(of_points[0])
    pick_points(1, 0, 1)
    next(of_points[0])
    pick_points(1, 1, 2)
    next(of_points[1])
    next(of_batch)
    next(of_points[1])
    for at in range(0, rows, CHUNK):
        to = slice(at, min(at + CHUNK, rows))
        form = augmented(centres[:, to], True)
        left[:, to] = form.astype(BF16)
        left_rows[to, :] = form.T.astype(BF16)
    for i in (1, 2, 5, 6):
        loads[i].wait()
    pairs[...] = paired(weights[...])
    eig_pair[0], eig_pair[1] = [part.astype(BF16) for part in pieces(eig[...], 2)]
    eig_turned[0], eig_turned[1] = [part.astype(BF16) for part in pieces(eig[...].T, 2)]
    next(of_points[0])
    next(of_batch)
    if by_block:
        for first, half in ((True, k), (False, 1 - k)):
            if not first:
                next(of_batch, None)
            blocks = [b_bufs[4].at[half, spot] for spot in range(xs)]
            get = [lambda t, ref=ref: ref[spot_in(ref.shape[:-2], t)[1]] for ref in blocks]
            feats = jnp.concatenate([load_tiles(one, high, 0, 1) for one in get], axis=1)
            part = kmul(left_rows, augmented(feats, False).astype(BF16), pairs)
            for spot in range(xs):
                into = p_bufs[0].at[1 - half, spot]

                def put(t, tile):
                    into[spot_in(into.shape[:-2], t)[1]] = tile

                store_tiles(part[:, spot * 128 : spot * 128 + 128], 0, put)
            if first:
                next(of_pred)
    else:
        next(of_batch, None)
        feats = load_all(b_bufs[4], high, 0, batch // 128)
        store_all(p_bufs[0], 0, kmul(left_rows, augmented(feats, False).astype(BF16), pairs), by_block)
        next(of_pred)
    next(of_pred)
    next(of_points[1])
    next(of_points[0])
    feats = load_all(b_bufs[4], high, 0, batch // 128)
    form = augmented(feats, False)
    batch_left[...] = augmented(feats, True).T.astype(BF16)
    keep_kernel(0, form.T.astype(BF16))
    next(of_pred)
    next(of_points[1])
    next(of_points[0])
    next(of_points[1])
    next(of_points[0])
    own_form(0)
    next(of_pred)
    point_form(0, k, x)
    next(of_points[1])
    own_form(1)
    next(of_pred, None)

    rest = load_all(p_bufs[4], outs // 8, 0, batch // 128, by_block) - targets[...]
    residual[...] = rest
    pair_rest = paired(rest)
    grad = jnp.dot(pair_rest, block_high[...], preferred_element_type=F32)
    grad = grad + jnp.dot(pair_rest, block_low[...], preferred_element_type=F32)
    m_bufs[0][...] = apply(grad[:outs] + grad[outs:], eig_pair, (((1,), (0,)), ((), ())))
    of_modes = mode_steps(place, m_bufs, m_sems, scale, eig_turned)
    next(of_modes)
    next(of_points[0])
    fold(paired(learning_rate * rest), 0, True)
    point_form(1, k, x)
    for spot in place.senders():
        point_form(0, k, spot)
    next(of_points[1])
    next(of_modes)
    for spot in place.senders():
        point_form(1, k, spot)
    next(of_points[0], None)
    for spot in range(xs):
        point_form(0, 1 - k, spot)
    next(of_points[1], None)
    for spot in range(xs):
        point_form(1, 1 - k, spot)
    next(of_modes, None)
    spread(place, m_bufs[4], by_line, m_bufs[3], spread_sems, use)


def local(xs, cs, centres, weights, targets, batch_index, nystrom_index, eigvecs, mode_scale):
    rows, width = centres.shape
    batch, outs = targets.shape
    points = nystrom_index.shape[0]
    block, modes = eigvecs.shape
    deep = depth_of(width)
    total = batch + points
    mode_share = -(-(outs // 8 * block // 128) // cs)
    piece = (mode_share, 8, 128)
    sems = [1] * 2 * (4 + 4 + 2 + 7 * HALVES)
    sems = sems + [cs - 1, 1, HALVES, 1, HALVES, 1, HALVES, 1, 7]
    arrays = [
        centres.T,
        weights.T,
        targets.T,
        batch_index[None, :],
        nystrom_index[None, :],
        mode_scale[None, :],
        eigvecs,
    ]
    residual, step = pl.pallas_call(
        functools.partial(main_body, xs, cs, batch, points),
        out_shape=[pltpu.VMEM((outs, batch), F32), pltpu.VMEM((outs, rows), F32)],
        in_specs=[pl.BlockSpec(memory_space=pl.ANY)] * 7,
        out_specs=[VMEM] * 2,
        scratch_shapes=everywhere_shapes(width // 8 * batch // 128, xs, cs)
        + everywhere_shapes(outs // 8 * batch // 128, xs, cs)
        + [
            pltpu.VMEM((outs, modes), F32),
            pltpu.VMEM((CORES * xs - 1, outs, modes), F32),
            pltpu.VMEM((cs,) + piece, F32),
            pltpu.VMEM((cs - 1,) + piece, F32),
            pltpu.VMEM((CORES, xs, cs) + piece, F32),
        ]
        + point_shapes(width // 8 * points // HALVES // 128, xs, cs) * HALVES
        + [
            pltpu.VMEM((3 * width, rows), BF16),
            pltpu.VMEM((rows, deep), BF16),
            pltpu.VMEM((batch, deep), BF16),
            pltpu.VMEM((batch, block), BF16),
            pltpu.VMEM((batch, block), BF16),
            pltpu.VMEM((2 * outs, rows), BF16),
            pltpu.VMEM((deep, rows), BF16),
            pltpu.VMEM((total, rows), BF16),
            pltpu.VMEM((total, rows), BF16),
        ]
        + [pltpu.SemaphoreType.DMA((n,)) for n in sems]
        + [pltpu.VMEM((xs - 1, cs) + piece, F32)]
        + [pltpu.VMEM(array.shape, array.dtype) for array in arrays]
        + [pltpu.VMEM((2, block, modes), BF16), pltpu.VMEM((2, modes, block), BF16)],
        compiler_params=pltpu.CompilerParams(
            collective_id=0, has_side_effects=True, vmem_limit_bytes=65_500_000
        ),
    )(*arrays)
    return (residual.T, step.T)


def solution(mesh):
    in_specs = (
        P(("row", "col"), None),
        P(("row", "col"), None),
        P(),
        P(),
        P(),
        P("row", "col"),
        P("col"),
    )
    out_specs = (P(), P(("row", "col"), None))
    body = functools.partial(local, mesh.shape["row"] // CORES, mesh.shape["col"])
    return jax.shard_map(body, mesh=mesh, in_specs=in_specs, out_specs=out_specs, check_vma=False)
```
